256 devices in a mesh: ex: 16 (over y_hi, x, core), co: 16 (over y_lo, z).
Axes of the slice: x: 4, y: 4 (y_hi: 2, y_lo: 2; y = y_hi * 2 + y_lo), z: 8, core: 2. Of those that a mesh axis runs over, the one named last changes fastest.
Arguments:
- train_grads: float32 [16384, 32768], P('ex', 'co')
- queries: float32 [1024, 32768], P('ex', 'co'), may hold values from -6 to 6
- module_ids: int32 [8], replicated, may hold values from 0 to 223
- module_scale: float32 [224], replicated, may hold values from 0.3 to 3
- example_ids: int32 [16384], P('ex'), may hold values from 0 to 16383, as said below
Outputs:
- influence: float32 [1024, 16384], P('co', 'ex')
The draws below stay inside these ranges and needn't reach their ends.
Inputs may be any that keep to these rules, and one draw needn't show every extreme that they name: `example_ids`: the examples of block s of 1024 rows carry the ids s * 1024 to (s + 1) * 1024 - 1, each once.
All inputs are finite; a program needn't handle non-finite values.
Results may differ from the reference program's by a relative error of at most 0.00008.
Values sent between devices are 32-bit elements; how exact they have to be, the bound alone decides.
No kernel may reach another device: no remote copies, remote signals or barrier semaphores. Data moves between devices by JAX's collectives and lax.ppermute only.
A program may use at most 128 MiB of HBM per device.

```python
import math
import jax
import jax.numpy as jnp
from jax import lax

PROJ = 4096
TOTAL_MODS = 224
MODS = 8
E_DEV = 1024
QUERIES = 1024
COORD = 32768
EXAMPLES = 16384


def draw_train_grads(key, part):
    key_row, key_col, key_main = jax.random.split(key, 3)
    row_scale = jnp.exp(jax.random.uniform(key_row, (EXAMPLES, 1), jnp.float32) * jnp.log(10.0))
    col_scale = jnp.exp(jax.random.uniform(key_col, (1, COORD), jnp.float32) * jnp.log(10.0))
    growth = (jnp.arange(COORD, dtype=jnp.float32) / COORD)[None, :]
    growth = jnp.exp(growth * jnp.log(3.0))
    entries = jax.random.normal(key_main, (EXAMPLES, COORD), jnp.float32)
    return (entries * row_scale * col_scale * growth / jnp.sqrt(jnp.float32(COORD))).astype(jnp.float32)


def shuffle_block(block_key):
    return jax.random.permutation(block_key, E_DEV)


def draw_example_ids(key, part):
    shards = EXAMPLES // E_DEV
    shard_keys = jax.random.split(jax.random.fold_in(key, 7), shards)
    shuffled = jax.vmap(shuffle_block)(shard_keys).astype(jnp.int32)
    offsets = (jnp.arange(shards, dtype=jnp.int32) * E_DEV)[:, None]
    return (shuffled + offsets).reshape(-1).astype(jnp.int32)


def place_ends(drawn, stream_key, least, high):
    extent = drawn.shape
    spot = [jax.random.randint(jax.random.fold_in(stream_key, axis), (), 0, extent[axis]) for axis in range(len(extent))]
    drawn = drawn.at[tuple(spot)].set(least)
    longest = extent.index(max(extent))
    spot[longest] = (spot[longest] + 1) % extent[longest]
    return drawn.at[tuple(spot)].set(high)


def with_spikes(values, key, source, target, blocks, factor):
    def block_of(dim):
        return (jnp.arange(values.shape[dim]) // (values.shape[dim] // blocks)).reshape((-1,) + (1,) * (values.ndim - 1 - dim))

    near = jax.random.permutation(key, blocks)[block_of(target)]
    second = (block_of(target) + blocks // 2) % blocks
    return jnp.where((block_of(source) == near) | (block_of(source) == second), factor * values, values)


def levels(stream_key, dims, cuts, low, largest):
    factor_of, own = 1.0, jax.random.fold_in(stream_key, 6)
    for dim, parts in cuts:
        draws = jnp.exp(jax.random.uniform(jax.random.fold_in(own, dim), (parts,), jnp.float32, low / len(cuts), largest / len(cuts)))
        factor_of = factor_of * jnp.repeat(draws, dims[dim] // parts).reshape([-1 if axis == dim else 1 for axis in range(len(dims))])
    return factor_of


def heavy_noise(stream_key, dims, width, bound, cuts, heavy, kind=jnp.bfloat16):
    array = width * jax.random.normal(stream_key, dims, jnp.float32)
    if cuts:
        array = array * levels(stream_key, dims, cuts, -0.22, 0.18)
    return jnp.clip(with_spikes(array, jax.random.fold_in(stream_key, 3), *heavy), -bound, bound).astype(kind)


def setup_inputs(seed: int = 0) -> dict:
    splits = jax.random.split(jax.random.key(seed), 6)
    return {
        "train_grads": draw_train_grads(jax.random.fold_in(splits[5], 71), 0),
        "queries": heavy_noise(splits[1], (QUERIES, COORD), 1.0, 6.0, ((0, 16), (1, 16)), (1, 0, 16, 2.0), jnp.float32),
        "module_ids": place_ends(jax.random.randint(splits[2], (MODS,), 0, TOTAL_MODS), jax.random.fold_in(splits[2], 1), 0, TOTAL_MODS - 1).astype(jnp.int32),
        "module_scale": jnp.clip(jnp.exp(jax.random.uniform(splits[3], (TOTAL_MODS,), jnp.float32, math.log(0.3), math.log(3.0))), 0.3, 3.0),
        "example_ids": draw_example_ids(jax.random.fold_in(splits[5], 71), 0),
    }


epsilon = 1e-06

def reference(train_grads, queries, module_ids, module_scale, example_ids):
    table_index = lax.iota(jnp.int32, module_scale.shape[0])
    picked = lax.optimization_barrier(jnp.sum(jnp.where(module_ids[:, None] == table_index[None, :], module_scale[None, :], jnp.zeros((), module_scale.dtype)), axis=1))
    position = lax.iota(jnp.int32, COORD)
    coord_scale = picked[(position // PROJ).astype(jnp.int32)]
    scaled = queries * coord_scale[None, :]
    squares = lax.optimization_barrier(jnp.sum(train_grads * train_grads, axis=1))
    inverse_norm = lax.rsqrt(squares + epsilon)
    raw_scores = lax.dot_general(scaled, train_grads, (((1,), (1,)), ((), ())), precision=lax.Precision.HIGHEST, preferred_element_type=jnp.float32)
    normed = raw_scores * inverse_norm[None, :]
    return jnp.zeros_like(normed).at[:, example_ids].set(normed)
```

```python
import jax
import jax.numpy as jnp
from jax import lax
from jax.sharding import PartitionSpec as P

PROJ = 4096
CHUNKS = 4
epsilon = 1e-06


def shards(train_grads, queries, module_ids, module_scale, example_ids):
    example_count, coord_count = train_grads.shape
    offset = lax.axis_index("co") * coord_count
    position = offset + lax.iota(jnp.int32, coord_count)
    table_index = lax.iota(jnp.int32, module_scale.shape[0])
    picked = jnp.sum(
        jnp.where(module_ids[:, None] == table_index[None, :], module_scale[None, :], 0.0), axis=1
    )
    window_index = lax.iota(jnp.int32, module_ids.shape[0])
    coord_scale = jnp.sum(
        jnp.where((position // PROJ)[:, None] == window_index[None, :], picked[None, :], 0.0), axis=1
    )
    scaled = queries * coord_scale[None, :]
    squares = jnp.sum(train_grads * train_grads, axis=1)
    norm_total = lax.all_gather(squares, "co").sum(0)
    inverse_norm = lax.rsqrt(norm_total + epsilon)
    rows = queries.shape[0] // CHUNKS
    outs = []
    for k in range(CHUNKS):
        all_q = lax.all_gather(scaled[k * rows:(k + 1) * rows], "ex", axis=0, tiled=True)
        s = lax.dot_general(all_q, train_grads, (((1,), (1,)), ((), ())),
                            precision=lax.Precision.HIGH, preferred_element_type=jnp.float32)
        outs.append(lax.psum_scatter(s, "co", scatter_dimension=0, tiled=True))
    own = jnp.concatenate(outs, 0)
    normed = own * inverse_norm[None, :]
    local_ids = example_ids - lax.axis_index("ex") * example_count
    return jnp.zeros_like(normed).at[:, local_ids].set(normed)


def solution(mesh):
    return jax.shard_map(shards, mesh=mesh,
        in_specs=(P("ex", "co"), P("ex", "co"), P(), P(), P("ex")),
        out_specs=P("co", "ex"), check_vma=False)
```

```python
import functools

import jax
import jax.numpy as jnp
from jax import lax
from jax.experimental import pallas as pl
from jax.experimental.pallas import tpu as pltpu
from jax.sharding import PartitionSpec as P

PROJ = 4096
EPSILON = 1e-06
BF, F32 = jnp.bfloat16, jnp.float32
NT = (((1,), (1,)), ((), ()))
NN = (((1,), (0,)), ((), ()))

YH, X, CORES, YL, Z = 2, 4, 2, 2, 8


def ex_index(yh, x, core):
    return ((yh % YH) * X + x % X) * CORES + core % CORES


def ex_perm(move):
    spots = [(yh, x, k) for yh in range(YH) for x in range(X) for k in range(CORES)]
    return [(ex_index(*s), ex_index(*move(*s))) for s in spots]


def co_perm(move):
    spots = [(yl, z) for yl in range(YL) for z in range(Z)]
    return [(yl * Z + z, (lambda a, b: (a % YL) * Z + b % Z)(*move(yl, z))) for yl, z in spots]


SWAP_CORE = ex_perm(lambda yh, x, k: (yh, x, 1 - k))
SWAP_YH = ex_perm(lambda yh, x, k: (1 - yh, x, k))
UP_X = ex_perm(lambda yh, x, k: (yh, x + 1, k))
DOWN_X = ex_perm(lambda yh, x, k: (yh, x - 1, k))
FAR_X = ex_perm(lambda yh, x, k: (yh, x + 2, k))
SWAP_YL = co_perm(lambda yl, z: (1 - yl, z))
UP_Z = co_perm(lambda yl, z: (yl, z + 1))
DOWN_Z = co_perm(lambda yl, z: (yl, z - 1))


def dot(a, b, dims):
    return lax.dot_general(a, b, dims, preferred_element_type=F32)


def split(x):
    hi = lax.reduce_precision(x, 8, 7)
    return hi.astype(BF), (x - hi).astype(BF)


def pack_kernel(count, scale_ref, *refs):
    rows = refs[0].shape[0]
    for i in range(count):
        q = refs[i][...] * scale_ref[0]
        hi = q.astype(BF)
        refs[count][i * rows:(i + 1) * rows, :] = hi
        refs[count + 1][i * rows:(i + 1) * rows, :] = (q - hi.astype(F32)).astype(BF)


def pack(scale, pieces):
    rows, c = pieces[0].shape
    vmem = pl.BlockSpec(memory_space=pltpu.VMEM)
    return pl.pallas_call(
        functools.partial(pack_kernel, len(pieces)),
        in_specs=[pl.BlockSpec(memory_space=pltpu.SMEM)] + [vmem] * len(pieces),
        out_specs=[vmem] * 2,
        out_shape=[jax.ShapeDtypeStruct((len(pieces) * rows, c), BF)] * 2,
        compiler_params=pltpu.CompilerParams(vmem_limit_bytes=16 << 20),
        name="pack",
    )(scale, *pieces)


def score(scale, hi, lo, *pieces):
    q_hi, q_lo = pack(scale, pieces)
    return dot(q_hi, hi, NT) + dot(q_hi, lo, NT) + dot(q_lo, hi, NT)


def core_swap(x):
    return lax.ppermute(x, "ex", SWAP_CORE)


class Order:
    def __init__(self):
        self.last = ()

    def gate(self, *args):
        return lax.optimization_barrier((*args, *self.last))[:len(args)]

    def run(self, f, *args):
        got = lax.optimization_barrier((*args, *self.last))[:len(args)]
        outs = f(*got)
        outs = outs if isinstance(outs, (tuple, list)) else (outs,)
        self.last = tuple(outs)
        return outs if len(outs) > 1 else outs[0]


class Scatter:
    def __init__(self, groups, spots, rows, more_up):
        self.groups, self.spots, self.rows = groups, spots, rows
        self.d, self.below, self.above = 4, None, None
        self.up, self.down = (4, 3) if more_up else (3, 4)

    def block(self, groups, k):
        spot, first, part = self.spots[k], 0, None
        for group in groups:
            count = group.shape[0] // self.rows
            at = jnp.clip(spot - first, 0, count - 1) * self.rows
            block = lax.dynamic_slice(group, (at, 0), (self.rows, group.shape[1]))
            part = block if part is None else jnp.where(spot < first, part, block)
            first += count
        return part

    def hop(self, order):
        d = self.d
        jobs = [(d, self.below)] * (d <= self.up) + [(Z - d, self.above)] * (d <= self.down)
        come = [v for _, v in jobs if v is not None]

        def pay(*vals):
            groups, came = vals[:len(self.groups)], list(vals[len(self.groups):])
            outs = []
            for k, v in jobs:
                own = self.block(groups, k)
                outs.append(own if v is None else own + came.pop(0))
            return outs

        outs = order.run(pay, *self.groups, *come)
        outs = list(outs) if isinstance(outs, (tuple, list)) else [outs]
        if d <= self.up:
            self.below = lax.ppermute(outs.pop(0), "co", UP_Z)
        if d <= self.down:
            self.above = lax.ppermute(outs.pop(0), "co", DOWN_Z)
        self.d -= 1

    def total(self):
        return self.block(self.groups, 0) + self.below + self.above


def shift_z(v, by):
    return lax.ppermute(v, "co", co_perm(lambda yl, z: (yl, z + by)))


def shards(train_grads, queries, module_ids, module_scale, example_ids):
    n, c = train_grads.shape
    ex, co = lax.axis_index("ex"), lax.axis_index("co")
    yh, x, core = ex >> 3, (ex >> 1) & 3, ex & 1
    yl, z = co >> 3, co & 7
    same = yl == yh
    owner = [(z + k) & 7 for k in range(Z)]
    away = [((w >> 1) - x) & 3 for w in owner]
    spots = [jnp.where(a == 0, 0, jnp.where(a == 1, 4, jnp.where(a == 2, 6, 2))) + ((w & 1) ^ core) for w, a in zip(owner, away)]
    order = Order()

    def pick(ids, table_ids, table):
        module = lax.dynamic_slice(ids, ((co * c) // PROJ,), (1,))
        hit = lax.iota(jnp.int32, table.shape[0]) == module
        scale = jnp.sum(jnp.where(hit, table, 0.0)).reshape(1)
        onehot = (lax.iota(jnp.int32, n)[:, None] == (table_ids - ex * n)[None, :]).astype(F32).astype(BF)
        return scale, onehot

    def halves(grads):
        hi, lo = split(grads)
        return hi, lo, jnp.sum(grads * grads, axis=1)

    def add(a, b):
        return a + b

    def place(onehot, rows):
        hi = lax.reduce_precision(rows, 8, 7)
        mid = lax.reduce_precision(rows - hi, 8, 7)
        terms = jnp.concatenate([hi, mid, rows - hi - mid], 0).astype(BF)
        moved = dot(terms, onehot, NT)
        m = rows.shape[0]
        return moved[:m] + moved[m:2 * m] + moved[2 * m:]

    own, rows = queries, queries.shape[0]
    up = lax.ppermute(queries, "ex", UP_X)
    down = lax.ppermute(queries, "ex", DOWN_X)
    own_x = core_swap(queries)
    theirs = lax.ppermute(queries, "ex", SWAP_YH)
    far = lax.ppermute(queries, "ex", FAR_X)
    hi, lo, sq = order.run(halves, train_grads)
    norm = shift_z(sq, 1)
    scale, onehot = order.run(pick, module_ids, example_ids, module_scale)
    up, down, theirs = order.gate(up, down, theirs)
    up_x, down_x, theirs_x = core_swap(up), core_swap(down), core_swap(theirs)
    up_b, down_b = lax.ppermute(theirs, "ex", UP_X), lax.ppermute(theirs, "ex", DOWN_X)
    sq = order.run(add, sq, norm)
    norm = shift_z(sq, 2)
    a0 = order.run(score, scale, hi, lo, own, own_x, up, up_x, down, down_x)
    (far,) = order.gate(far)
    far_x, far_b = core_swap(far), lax.ppermute(far, "ex", SWAP_YH)
    sq = order.run(add, sq, norm)
    norm = shift_z(sq, 4)
    a1 = order.run(score, scale, hi, lo, far, far_x)
    za = Scatter((a0, a1), spots, rows, True)
    za.hop(order)
    up_b, down_b = order.gate(up_b, down_b)
    up_bx, down_bx = core_swap(up_b), core_swap(down_b)
    sq = order.run(add, sq, norm)
    norm = lax.ppermute(sq, "co", SWAP_YL)
    za.hop(order)
    (far_b,) = order.gate(far_b)
    far_bx = core_swap(far_b)
    b0 = order.run(score, scale, hi, lo, theirs, theirs_x, up_b, up_bx, down_b, down_bx, far_b, far_bx)
    zb = Scatter((b0,), spots, rows, False)
    zb.hop(order)
    za.hop(order)
    zb.hop(order)
    za.hop(order)
    inverse_norm = order.run(lambda s, n: lax.rsqrt(s + n + EPSILON), sq, norm)
    zb.hop(order)
    za_total = order.run(lambda *v: za.block(v[:2], 0) + v[2] + v[3], *za.groups, za.below, za.above)
    zb.hop(order)
    zb_total = zb.total()
    got = lax.ppermute(jnp.where(same, zb_total, za_total), "co", SWAP_YL)
    return place(onehot, (jnp.where(same, za_total, zb_total) + got) * inverse_norm[None, :])


def solution(mesh):
    return jax.shard_map(
        shards,
        mesh=mesh,
        in_specs=(P("ex", "co"), P("ex", "co"), P(), P(), P("ex")),
        out_specs=P("co", "ex"),
        check_vma=False,
    )
```
